32 devices in a mesh: ty: 4 (over y, core), tx: 8 (over z, x).
Axes of the slice: x: 2, y: 2, z: 4, core: 2. Of those that a mesh axis runs over, the one named last changes fastest.
Arguments:
- object_field: float32 [2, 2, 1536, 3072], P(None, None, 'ty', 'tx'), may hold values from -5 to 5
- probe_wave: float32 [2, 256, 256], replicated, may hold values from -6 to 6
- prop_phase: float32 [256, 256], replicated, may hold values from -3.140625 to 3.140625
- amplitude: float32 [128, 256, 256], P(('ty', 'tx')), may hold values from 0.1 to 3
- offsets: int32 [2, 128], P(None, ('ty', 'tx')), may hold values from 0 to 383, as said below
- live_slots: int32 [128], P(('ty', 'tx')), may hold values from 0 to 1, as said below
Outputs:
- object_grad: float32 [2, 2, 1536, 3072], P(None, None, 'ty', 'tx')
- probe_grad: float32 [2, 256, 256], replicated
The draws below stay inside these ranges and needn't reach their ends.
Inputs may be any that keep to these rules, and one draw needn't show every extreme that they name: `offsets`: offsets of row and column of a window inside its device's tile; on devices of the last row of ty the row offset is at most 128, on the last column of tx the column offset likewise, so every window lies inside the object. `live_slots`: each device has between 1 and 4 live slots, in any of its slots; some device has exactly 4.
All inputs are finite; a program needn't handle non-finite values.
Results may differ from the reference program's by a relative error of at most 0.0003.
Values sent between devices are 32-bit elements; how exact they have to be, the bound alone decides.
No kernel may reach another device: no remote copies, remote signals or barrier semaphores. Data moves between devices by JAX's collectives and lax.ppermute only.
A program may use at most 128 MiB of HBM per device.

```python
import math
import jax
import jax.numpy as jnp
from jax import lax

PATCH = 256
SLICES = 2
TILE = 384
MAXPOS = 4
OY = 1536
OX = 3072
SLOTS = 128
N_TY = 4
N_TX = 8


def draw_offsets(key, part):
    slots = MAXPOS * N_TY * N_TX
    keys = jax.random.split(jax.random.fold_in(key, 11), 4)
    slot_ids = jnp.arange(slots, dtype=jnp.int32)
    device = slot_ids // MAXPOS
    row_ids = device // N_TX
    col_ids = device % N_TX
    inner = jax.random.randint(keys[0], (2, slots), 0, TILE, dtype=jnp.int32)
    edged = jax.random.randint(keys[1], (2, slots), 0, TILE - PATCH + 1, dtype=jnp.int32)
    at_edge = jnp.stack([row_ids == N_TY - 1, col_ids == N_TX - 1])
    chosen = jnp.where(at_edge, edged, inner)
    pick_row = jax.random.randint(keys[2], (), 0, N_TY - 1, dtype=jnp.int32)
    pick_col = jax.random.randint(keys[3], (), 0, N_TX - 1, dtype=jnp.int32)
    target = (pick_row * N_TX + pick_col) * MAXPOS
    chosen = chosen.at[:, target].set(TILE - 1)
    chosen = chosen.at[:, target + 1].set(0)
    return chosen.astype(jnp.int32)


def draw_live_slots(key, part):
    devices = N_TY * N_TX
    keys = jax.random.split(jax.random.fold_in(key, 23), 3)
    counts = jax.random.randint(keys[0], (devices,), 1, MAXPOS + 1, dtype=jnp.int32)
    busiest = jax.random.randint(keys[1], (), 0, devices, dtype=jnp.int32)
    counts = counts.at[busiest].set(MAXPOS)
    scores = jax.random.randint(keys[2], (devices, MAXPOS), 0, 1 << 20, dtype=jnp.int32) * MAXPOS
    scores = scores + jnp.arange(MAXPOS, dtype=jnp.int32)[None, :]
    ranks = jnp.argsort(jnp.argsort(scores, axis=1), axis=1)
    return (ranks < counts[:, None]).astype(jnp.int32).reshape(-1)


def block_scale(key, shape, cuts, smallest, largest):
    gain = 1.0
    for position, blocks in cuts:
        steps = jax.random.uniform(jax.random.fold_in(jax.random.fold_in(key, 6), position), (blocks,), jnp.float32, smallest / len(cuts), largest / len(cuts))
        gain = gain * jnp.repeat(jnp.exp(steps), shape[position] // blocks).reshape((-1,) + (1,) * (len(shape) - 1 - position))
    return gain


def gaussian(rng, extent, scale, bound, cuts=(), kind=jnp.bfloat16):
    values = jax.random.normal(rng, extent, jnp.float32) * scale
    if len(cuts) > 0:
        values = block_scale(rng, extent, cuts, -0.22, 0.18) * values
    return jnp.clip(values, min=-bound, max=bound).astype(kind)


def setup_inputs(seed: int = 0) -> dict:
    key_of = jax.random.split(jax.random.key(seed), 7)
    return {
        "object_field": gaussian(key_of[0], (SLICES, 2, OY, OX), 0.7, 5.0, ((2, 4), (3, 8)), jnp.float32),
        "probe_wave": gaussian(key_of[1], (2, PATCH, PATCH), 1.0, 6.0, (), jnp.float32),
        "prop_phase": jnp.clip(jax.random.uniform(key_of[2], (PATCH, PATCH), jnp.float32, -3.140625, 3.140625), -3.140625, 3.140625),
        "amplitude": jnp.clip(jnp.exp(math.log(3.0) - 3.4011974 * jax.random.uniform(key_of[3], (SLOTS, PATCH, PATCH), jnp.float32) ** block_scale(key_of[3], (SLOTS, PATCH, PATCH), ((0, 32),), -0.2, 0.2)), 0.1, 3.0),
        "offsets": draw_offsets(jax.random.fold_in(key_of[6], 71), 0),
        "live_slots": draw_live_slots(jax.random.fold_in(key_of[6], 71), 0),
    }


def dft_tables(length):
    indices = jnp.arange(length, dtype=jnp.int32)
    product = indices[:, None] * indices[None, :] % length
    angles = product.astype(jnp.float32) * (2.0 * math.pi / length)
    factor = 1.0 / math.sqrt(length)
    return (jnp.cos(angles) * factor, jnp.sin(angles) * factor)

def matmul(left, right):
    return jnp.dot(left, right, precision=lax.Precision.HIGHEST, preferred_element_type=jnp.float32)

def transform(real_part, imag_part, cosine, sine_table, orient):
    half_real = matmul(real_part, cosine) - orient * matmul(imag_part, sine_table)
    half_imag = matmul(imag_part, cosine) + orient * matmul(real_part, sine_table)
    full_real = matmul(cosine, half_real) - orient * matmul(sine_table, half_imag)
    full_imag = matmul(cosine, half_imag) + orient * matmul(sine_table, half_real)
    return (full_real, full_imag)

def patch_gradient(window, probe_wave, prop_real, prop_imag, measured, cosine, sine_table):
    layers = window.shape[0]
    wave_real, wave_imag = (probe_wave[0], probe_wave[1])
    incident = []
    for layer_index in range(layers):
        trans_real, trans_imag = (window[layer_index, 0], window[layer_index, 1])
        incident.append((wave_real, wave_imag))
        exit_real = trans_real * wave_real - trans_imag * wave_imag
        exit_imag = trans_real * wave_imag + trans_imag * wave_real
        freq_real, freq_imag = transform(exit_real, exit_imag, cosine, sine_table, -1.0)
        if layer_index + 1 < layers:
            kept_real = prop_real * freq_real - prop_imag * freq_imag
            kept_imag = prop_real * freq_imag + prop_imag * freq_real
            wave_real, wave_imag = transform(kept_real, kept_imag, cosine, sine_table, 1.0)
    modulus = jnp.sqrt(freq_real * freq_real + freq_imag * freq_imag + 0.25)
    factor = measured / modulus - 1.0
    back_real, back_imag = transform(freq_real * factor, freq_imag * factor, cosine, sine_table, 1.0)
    pieces = [None] * layers
    probe_real, probe_imag = (back_real, back_imag)
    for layer_index in reversed(range(layers)):
        inc_real, inc_imag = incident[layer_index]
        trans_real, trans_imag = (window[layer_index, 0], window[layer_index, 1])
        pieces[layer_index] = jnp.stack([inc_real * back_real + inc_imag * back_imag, inc_real * back_imag - inc_imag * back_real])
        delta_real = trans_real * back_real + trans_imag * back_imag
        delta_imag = trans_real * back_imag - trans_imag * back_real
        if layer_index > 0:
            upper_real, upper_imag = transform(delta_real, delta_imag, cosine, sine_table, -1.0)
            moved_real = prop_real * upper_real + prop_imag * upper_imag
            moved_imag = prop_real * upper_imag - prop_imag * upper_real
            back_real, back_imag = transform(moved_real, moved_imag, cosine, sine_table, 1.0)
        else:
            probe_real, probe_imag = (delta_real, delta_imag)
    return (jnp.stack(pieces), jnp.stack([probe_real, probe_imag]))

def reference(object_field, probe_wave, prop_phase, amplitude, offsets, live_slots):
    cosine, sine_table = dft_tables(PATCH)
    prop_real = jnp.cos(prop_phase)
    prop_imag = jnp.sin(prop_phase)
    anchor = jnp.zeros((), jnp.int32)

    def visit(carry, slot_index):
        gradient, probe_total = carry
        device = slot_index // MAXPOS
        row_start = (device // N_TX * TILE + offsets[0, slot_index]).astype(jnp.int32)
        col_start = (device % N_TX * TILE + offsets[1, slot_index]).astype(jnp.int32)
        corner = (anchor, anchor, row_start, col_start)
        window = lax.dynamic_slice(object_field, corner, (SLICES, 2, PATCH, PATCH))
        pieces, probe_piece = patch_gradient(window, probe_wave, prop_real, prop_imag, amplitude[slot_index], cosine, sine_table)
        weight = live_slots[slot_index].astype(jnp.float32)
        previous = lax.dynamic_slice(gradient, corner, (SLICES, 2, PATCH, PATCH))
        gradient = lax.dynamic_update_slice(gradient, previous + weight * pieces, corner)
        return ((gradient, probe_total + weight * probe_piece), None)
    initial = (jnp.zeros(object_field.shape, jnp.float32), jnp.zeros(probe_wave.shape, jnp.float32))
    (gradient, probe_total), ignored = lax.scan(visit, initial, jnp.arange(MAXPOS * N_TY * N_TX, dtype=jnp.int32))
    return (gradient, probe_total * (1.0 / math.sqrt(MAXPOS * N_TY * N_TX)))
```

```python
import functools
import math

import jax
import jax.numpy as jnp
import ml_dtypes
import numpy as np
from jax import lax
from jax.experimental import pallas as pl
from jax.experimental.pallas import tpu as pltpu
from jax.sharding import PartitionSpec as P

LANES = 128
SUBLANES = 8


def passed_along(block, axis, distance):
    devices = range(lax.axis_size(axis))
    route = [(i - distance, i) for i in devices if i - distance in devices]
    return lax.ppermute(block, axis, route)


def dft_tables(length):
    indices = np.arange(length)
    angles = (indices[:, None] * indices[None, :] % length) * (2.0 * math.pi / length)
    cosine = np.cos(angles) / math.sqrt(length)
    sine = np.sin(angles) / math.sqrt(length)
    parts = []
    for table in (cosine, cosine + sine, cosine - sine):
        high = table.astype(ml_dtypes.bfloat16)
        low = (table - high.astype(np.float64)).astype(ml_dtypes.bfloat16)
        parts.append(np.stack([high, low]))
    return np.stack(parts)


def split(x):
    high = x.astype(jnp.bfloat16)
    low = (x - high.astype(jnp.float32)).astype(jnp.bfloat16)
    return high, low


def right_product(x, tables, which):
    high, low = split(x)
    data = jnp.concatenate([high, low, high], axis=1)
    table = jnp.concatenate([tables[which, 0], tables[which, 0], tables[which, 1]], axis=0)
    return jnp.dot(data, table, preferred_element_type=jnp.float32)


def left_product(x, tables, which):
    high, low = split(x)
    data = jnp.concatenate([high, low, high], axis=0)
    table = jnp.concatenate([tables[which, 0], tables[which, 0], tables[which, 1]], axis=1)
    return jnp.dot(table, data, preferred_element_type=jnp.float32)


def transform(real, imag, tables, inverse):
    first, second = (1, 2) if inverse else (2, 1)
    for product in (right_product, left_product):
        shared = product(real + imag, tables, 0)
        real, imag = (
            shared - product(imag, tables, first),
            shared - product(real, tables, second),
        )
    return real, imag


def row_groups(block):
    return block.reshape(block.shape[0] // SUBLANES, SUBLANES, block.shape[1])


def read_window(ext, plane, row, col, patch):
    base_row = pl.multiple_of(row // SUBLANES * SUBLANES, SUBLANES)
    base_col = pl.multiple_of(col // LANES * LANES, LANES)
    down, right = row % SUBLANES, col % LANES
    tall = patch + SUBLANES
    wide = ext[plane, pl.ds(base_row, tall), pl.ds(base_col, patch + LANES)]
    turned = [
        pltpu.roll(wide[:, k * LANES : (k + 1) * LANES], (LANES - right) % LANES, 1)
        for k in range(patch // LANES + 1)
    ]
    keep = lax.broadcasted_iota(jnp.int32, (tall, LANES), 1) < LANES - right
    columns = []
    for k in range(patch // LANES):
        groups = row_groups(jnp.where(keep, turned[k], turned[k + 1]))
        groups = pltpu.roll(groups, (SUBLANES - down) % SUBLANES, 1)
        first = lax.broadcasted_iota(jnp.int32, (patch // SUBLANES, SUBLANES, LANES), 1)
        moved = jnp.where(first < SUBLANES - down, groups[:-1], groups[1:])
        columns.append(moved.reshape(patch, LANES))
    return jnp.concatenate(columns, axis=1)


def add_window(ext, plane, row, col, piece):
    patch = piece.shape[0]
    base_row = pl.multiple_of(row // SUBLANES * SUBLANES, SUBLANES)
    base_col = pl.multiple_of(col // LANES * LANES, LANES)
    down, right = row % SUBLANES, col % LANES
    tall = patch + SUBLANES
    blank = jnp.zeros((1, SUBLANES, LANES), jnp.float32)
    within = lax.broadcasted_iota(jnp.int32, (tall // SUBLANES, SUBLANES, LANES), 1) >= down
    turned = []
    for k in range(patch // LANES):
        groups = pltpu.roll(row_groups(piece[:, k * LANES : (k + 1) * LANES]), down, 1)
        moved = jnp.where(
            within,
            jnp.concatenate([groups, blank], axis=0),
            jnp.concatenate([blank, groups], axis=0),
        )
        turned.append(pltpu.roll(moved.reshape(tall, LANES), right, 1))
    keep = lax.broadcasted_iota(jnp.int32, (tall, LANES), 1) >= right
    zero = jnp.zeros((tall, LANES), jnp.float32)
    after, before = turned + [zero], [zero] + turned
    spread = jnp.concatenate(
        [jnp.where(keep, after[k], before[k]) for k in range(patch // LANES + 1)], axis=1
    )
    spot = (plane, pl.ds(base_row, tall), pl.ds(base_col, patch + LANES))
    ext[spot] = ext[spot] + spread


def fill_extended(layer, tile, patch, field, top, bottom, lower, corner, ext, sems):
    whole = slice(None)
    jobs = (
        (field.at[layer], ext.at[whole, :tile, :tile]),
        (top, ext.at[whole, :patch, tile:]),
        (bottom, ext.at[whole, patch:tile, tile:]),
        (lower, ext.at[whole, tile:, :tile]),
        (corner, ext.at[whole, tile:, tile:]),
    )
    copies = [pltpu.make_async_copy(a, b, sems.at[k]) for k, (a, b) in enumerate(jobs)]
    for copy in copies:
        copy.start()
    for copy in copies:
        copy.wait()


def drain_extended(tile, patch, ext, own, top, bottom, lower, corner, sems):
    whole = slice(None)
    jobs = (
        (ext.at[whole, tile:, tile:], corner),
        (ext.at[whole, patch:tile, tile:], bottom),
        (ext.at[whole, :patch, tile:], top),
        (ext.at[whole, tile:, :tile], lower),
        (ext.at[whole, :tile, :tile], own),
    )
    copies = [pltpu.make_async_copy(a, b, sems.at[k]) for k, (a, b) in enumerate(jobs)]
    for copy in copies:
        copy.start()
    for copy in copies:
        copy.wait()


def first_kernel(
    tile, patch, offsets, field, top, bottom, lower, corner, probe, prop, tables,
    window_out, wave_out, ext, sems,
):
    slot = pl.program_id(0)

    @pl.when(slot == 0)
    def _():
        fill_extended(0, tile, patch, field, top, bottom, lower, corner, ext, sems)

    row, col = offsets[0, slot], offsets[1, slot]
    trans_real = read_window(ext, 0, row, col, patch)
    trans_imag = read_window(ext, 1, row, col, patch)
    window_out[0, 0] = trans_real
    window_out[0, 1] = trans_imag
    wave_real, wave_imag = probe[0], probe[1]
    real, imag = transform(
        trans_real * wave_real - trans_imag * wave_imag,
        trans_real * wave_imag + trans_imag * wave_real,
        tables,
        False,
    )
    prop_real, prop_imag = prop[0], prop[1]
    real, imag = transform(
        prop_real * real - prop_imag * imag, prop_real * imag + prop_imag * real, tables, True
    )
    wave_out[0, 0] = real
    wave_out[0, 1] = imag


def second_kernel(
    tile, patch, offsets, live, field, top, bottom, lower, corner, wave, amplitude, tables,
    delta_out, own_out, top_out, bottom_out, lower_out, corner_out, ext, acc, sems,
):
    slot = pl.program_id(0)

    @pl.when(slot == 0)
    def _():
        fill_extended(1, tile, patch, field, top, bottom, lower, corner, ext, sems)
        acc[...] = jnp.zeros_like(acc)

    row, col = offsets[0, slot], offsets[1, slot]
    weight = live[slot].astype(jnp.float32)
    trans_real = read_window(ext, 0, row, col, patch)
    trans_imag = read_window(ext, 1, row, col, patch)
    wave_real, wave_imag = wave[0, 0], wave[0, 1]
    real, imag = transform(
        trans_real * wave_real - trans_imag * wave_imag,
        trans_real * wave_imag + trans_imag * wave_real,
        tables,
        False,
    )
    factor = amplitude[0] * lax.rsqrt(real * real + imag * imag + 0.25) - 1.0
    real, imag = transform(real * factor, imag * factor, tables, True)
    real, imag = real * weight, imag * weight
    delta_out[0, 0] = trans_real * real + trans_imag * imag
    delta_out[0, 1] = trans_real * imag - trans_imag * real
    add_window(acc, 0, row, col, wave_real * real + wave_imag * imag)
    add_window(acc, 1, row, col, wave_real * imag - wave_imag * real)

    @pl.when(slot == pl.num_programs(0) - 1)
    def _():
        drain_extended(
            tile, patch, acc, own_out, top_out, bottom_out, lower_out, corner_out, sems
        )


def third_kernel(
    tile, patch, scaling, offsets, delta, window, probe, prop, tables,
    probe_out, own_out, top_out, bottom_out, lower_out, corner_out, acc, sems,
):
    slot = pl.program_id(0)

    @pl.when(slot == 0)
    def _():
        acc[...] = jnp.zeros_like(acc)
        probe_out[...] = jnp.zeros_like(probe_out)

    row, col = offsets[0, slot], offsets[1, slot]
    real, imag = transform(delta[0, 0], delta[0, 1], tables, False)
    prop_real, prop_imag = prop[0], prop[1]
    real, imag = transform(
        prop_real * real + prop_imag * imag, prop_real * imag - prop_imag * real, tables, True
    )
    wave_real, wave_imag = probe[0], probe[1]
    add_window(acc, 0, row, col, wave_real * real + wave_imag * imag)
    add_window(acc, 1, row, col, wave_real * imag - wave_imag * real)
    trans_real, trans_imag = window[0, 0], window[0, 1]
    probe_out[0] += (trans_real * real + trans_imag * imag) * scaling
    probe_out[1] += (trans_real * imag - trans_imag * real) * scaling

    @pl.when(slot == pl.num_programs(0) - 1)
    def _():
        drain_extended(
            tile, patch, acc, own_out, top_out, bottom_out, lower_out, corner_out, sems
        )


ANY = pl.BlockSpec(memory_space=pl.ANY)
SCALARS = pl.BlockSpec(memory_space=pltpu.SMEM)


def whole_spec(array):
    return pl.BlockSpec(array.shape, lambda slot: (0,) * len(array.shape))


def slot_spec(shape):
    return pl.BlockSpec((1,) + tuple(shape[1:]), lambda slot: (slot,) + (0,) * (len(shape) - 1))


def part_shapes(tile, patch):
    sizes = ((tile, tile), (patch, patch), (tile - patch, patch), (patch, tile), (patch, patch))
    return [jax.ShapeDtypeStruct((2,) + size, jnp.float32) for size in sizes]


def kernel_cost(slots, patch, extra):
    return pl.CostEstimate(
        flops=slots * 2 * 2 * 3 * 3 * 2 * patch**3, bytes_accessed=extra, transcendentals=0
    )


def run_first(offsets, field, halo, probe, prop, tables):
    slots, tile, patch = offsets.shape[1], field.shape[2], probe.shape[1]
    reach = tile + patch
    stacked = jax.ShapeDtypeStruct((slots, 2, patch, patch), jnp.float32)
    return pl.pallas_call(
        functools.partial(first_kernel, tile, patch),
        grid=(slots,),
        in_specs=[SCALARS] + [ANY] * 5 + [whole_spec(a) for a in (probe, prop, tables)],
        out_specs=[slot_spec(stacked.shape)] * 2,
        out_shape=[stacked] * 2,
        scratch_shapes=[
            pltpu.VMEM((2, reach, reach), jnp.float32),
            pltpu.SemaphoreType.DMA((5,)),
        ],
        cost_estimate=kernel_cost(slots, patch, 8 << 20),
        name="first",
    )(offsets, field, *halo, probe, prop, tables)


def run_second(offsets, live, field, halo, wave, amplitude, tables):
    slots, tile, patch = offsets.shape[1], field.shape[2], wave.shape[2]
    reach = tile + patch
    return pl.pallas_call(
        functools.partial(second_kernel, tile, patch),
        grid=(slots,),
        in_specs=[SCALARS] * 2
        + [ANY] * 5
        + [slot_spec(wave.shape), slot_spec(amplitude.shape), whole_spec(tables)],
        out_specs=[slot_spec(wave.shape)] + [ANY] * 5,
        out_shape=[jax.ShapeDtypeStruct(wave.shape, jnp.float32)] + part_shapes(tile, patch),
        scratch_shapes=[
            pltpu.VMEM((2, reach, reach), jnp.float32),
            pltpu.VMEM((2, reach, reach), jnp.float32),
            pltpu.SemaphoreType.DMA((5,)),
        ],
        cost_estimate=kernel_cost(slots, patch, 12 << 20),
        name="second",
    )(offsets, live, field, *halo, wave, amplitude, tables)


def run_third(offsets, delta, window, probe, prop, tables, tile, scaling):
    slots, patch = offsets.shape[1], probe.shape[1]
    reach = tile + patch
    return pl.pallas_call(
        functools.partial(third_kernel, tile, patch, scaling),
        grid=(slots,),
        in_specs=[SCALARS]
        + [slot_spec(delta.shape), slot_spec(window.shape)]
        + [whole_spec(a) for a in (probe, prop, tables)],
        out_specs=[whole_spec(probe)] + [ANY] * 5,
        out_shape=[jax.ShapeDtypeStruct(probe.shape, jnp.float32)] + part_shapes(tile, patch),
        scratch_shapes=[
            pltpu.VMEM((2, reach, reach), jnp.float32),
            pltpu.SemaphoreType.DMA((5,)),
        ],
        cost_estimate=kernel_cost(slots, patch, 10 << 20),
        name="third",
    )(offsets, delta, window, probe, prop, tables)


def fetch_halo(local, layer, patch):
    tile = local.shape[2]
    top = passed_along(local[layer, :, :patch, :patch], "tx", -1)
    bottom = passed_along(local[layer, :, patch:tile, :patch], "tx", -1)
    lower = passed_along(local[layer, :, :patch, :], "ty", -1)
    corner = passed_along(top, "ty", -1)
    return top, bottom, lower, corner


def return_parts(parts, patch):
    own, top, bottom, lower, corner = parts
    corner = passed_along(corner, "ty", 1)
    bottom = passed_along(bottom, "tx", 1)
    lower = passed_along(lower, "ty", 1)
    top = passed_along(top + corner, "tx", 1)
    own = own.at[:, :patch, :].add(lower)
    own = own.at[:, :patch, :patch].add(top)
    return own.at[:, patch:, :patch].add(bottom)


def exchange_stages():
    columns, rows = lax.axis_size("tx"), lax.axis_size("ty")
    column_bits = [1 << b for b in range(columns.bit_length() - 1)]
    row_bits = [columns << b for b in range(rows.bit_length() - 1)]
    order = row_bits[:1]
    rest = row_bits[1:]
    while rest or column_bits:
        if rest:
            order.append(rest.pop(0))
        if column_bits:
            order.append(column_bits.pop(0))
    return [order[:1]] + [order[k : k + 2] for k in range(1, len(order), 2)]


def swapped(block, mask):
    count = lax.axis_size("ty") * lax.axis_size("tx")
    return lax.ppermute(block, ("ty", "tx"), [(i, i ^ mask) for i in range(count)])


def spread_sum(block):
    rows, columns = lax.axis_size("ty"), lax.axis_size("tx")
    if rows & (rows - 1) or columns & (columns - 1):
        return lax.psum(block, ("ty", "tx"))
    me = lax.axis_index("ty") * columns + lax.axis_index("tx")
    shape = block.shape
    current = block.reshape(-1, shape[-1])
    stages = exchange_stages()
    history = []
    for bits in stages[:-1]:
        masks = [sum(b for k, b in enumerate(bits) if m >> k & 1) for m in range(1 << len(bits))]
        place = sum(((me & b) != 0).astype(jnp.int32) << k for k, b in enumerate(bits))
        size = current.shape[0] // len(masks)
        total = lax.dynamic_slice_in_dim(current, place * size, size)
        for m in range(1, len(masks)):
            total = total + swapped(
                lax.dynamic_slice_in_dim(current, (place ^ m) * size, size), masks[m]
            )
        history.append((masks, place, size))
        current = total
    bits = stages[-1]
    masks = [sum(b for k, b in enumerate(bits) if m >> k & 1) for m in range(1 << len(bits))]
    got = [current] + [swapped(current, mask) for mask in masks[1:]]
    place = sum(((me & b) != 0).astype(jnp.int32) << k for k, b in enumerate(bits))
    current = sum(ordered(got, place))
    for masks, place, size in reversed(history):
        got = [current] + [swapped(current, mask) for mask in masks[1:]]
        current = jnp.concatenate(ordered(got, place), axis=0)
    return current.reshape(shape)


def ordered(got, place):
    bit = 1
    while bit < len(got):
        flip = (place & bit) != 0
        got = [jnp.where(flip, got[k ^ bit], got[k]) for k in range(len(got))]
        bit *= 2
    return got


def per_device(object_field, probe_wave, prop_phase, amplitude, offsets, live_slots):
    tile = object_field.shape[2]
    patch = probe_wave.shape[1]
    capacity = live_slots.shape[0]
    halo_first = fetch_halo(object_field, 0, patch)
    halo_second = fetch_halo(object_field, 1, patch)
    tables = jnp.asarray(dft_tables(patch))
    prop = jnp.stack([jnp.cos(prop_phase), jnp.sin(prop_phase)])
    window, wave = run_first(offsets, object_field, halo_first, probe_wave, prop, tables)
    delta, *parts_second = run_second(
        offsets, live_slots, object_field, halo_second, wave, amplitude, tables
    )
    scaling = 1.0 / math.sqrt(capacity * lax.axis_size("ty") * lax.axis_size("tx"))
    probe_sum, *parts_first = run_third(
        offsets, delta, window, probe_wave, prop, tables, tile, scaling
    )
    grad_second = return_parts(parts_second, patch)
    grad_first = return_parts(parts_first, patch)
    return jnp.stack([grad_first, grad_second]), spread_sum(probe_sum)


def solution(mesh):
    placed = (
        P(None, None, "ty", "tx"),
        P(),
        P(),
        P(("ty", "tx"), None, None),
        P(None, ("ty", "tx")),
        P(("ty", "tx")),
    )
    return jax.shard_map(
        per_device,
        mesh=mesh,
        in_specs=placed,
        out_specs=(P(None, None, "ty", "tx"), P()),
        check_vma=False,
    )
```
